32 devices in a mesh: seg: 8 (over z, x), sub: 4 (over y, core).
Axes of the slice: x: 2, y: 2, z: 4, core: 2. Of those that a mesh axis runs over, the one named last changes fastest.
Arguments:
- leaf_mult: float32 [32768, 256], P(('seg', 'sub')), may hold values from -6 to 6
- m2m_ops: float32 [8, 256, 256], replicated, may hold values from -0.125 to 0.125
- m2l_ops: float32 [32, 256, 256], replicated, may hold values from -0.0625 to 0.0625
- owner_box: int32 [4096], P(('seg', 'sub')), may hold values from 0 to 4095, as said below
- src_list: int32 [4096, 32], P(('seg', 'sub')), may hold values from -1 to 4095, as said below
Outputs:
- parent_mult: float32 [4096, 256], P(('seg', 'sub'))
- owned_mult: float32 [4096, 256], P(('seg', 'sub'))
- local_exp: float32 [4096, 256], P(('seg', 'sub'))
The draws below stay inside these ranges and needn't reach their ends.
Inputs may be any that keep to these rules, and one draw needn't show every extreme that they name: `owner_box`: each aligned block of 512 rows, the g-th, holds every box id from g * 512 to (g + 1) * 512 - 1 once. `src_list`: A slot of a row in the g-th aligned block of 512 rows is -1 or names a box of the blocks g - 1, g or g + 1 of Morton order, each block being 512 consecutive ids.
All inputs are finite; a program needn't handle non-finite values.
Results may differ from the reference program's by a relative error of at most 0.000082.
Values sent between devices are 32-bit elements; how exact they have to be, the bound alone decides.
A program may use at most 64 MiB of HBM per device.

```python
import jax
import jax.numpy as jnp
from jax import lax

K = 256
SLOTS = 32
GROUP = 512
PARENTS = 4096
LEAVES = 32768
N_SEG = 8


def draw_owner_box(key, part):
    group_keys = jax.random.split(jax.random.fold_in(key, 11), N_SEG)
    orders = jax.vmap(lambda one_key: jax.random.permutation(one_key, GROUP))(group_keys)
    starts = (jnp.arange(N_SEG, dtype=jnp.int32) * GROUP)[:, None]
    return (orders.astype(jnp.int32) + starts).reshape(PARENTS)


def draw_src_list(key, part):
    pick_key, live_key = jax.random.split(jax.random.fold_in(key, 23))
    group_of = jnp.arange(PARENTS, dtype=jnp.int32) // GROUP
    low_end = jnp.maximum(group_of - 1, 0) * GROUP
    high_end = jnp.minimum(group_of + 2, N_SEG) * GROUP
    spans = (high_end - low_end)[:, None]
    chosen = jax.random.randint(pick_key, (PARENTS, SLOTS), 0, 1 << 30, dtype=jnp.int32) % spans + low_end[:, None]
    present = jax.random.randint(live_key, (PARENTS, SLOTS), 0, 4, dtype=jnp.int32) < 3
    result = jnp.where(present, chosen, -1)
    result = result.at[0, SLOTS - 1].set(-1)
    result = result.at[PARENTS - 1, 0].set(PARENTS - 1)
    return result.astype(jnp.int32)


def block_scale(key, extent, cuts, smallest, top_value):
    gain, own = 1.0, jax.random.fold_in(key, 6)
    for position, shards_of in cuts:
        steps = jnp.exp(jax.random.uniform(jax.random.fold_in(own, position), (shards_of,), jnp.float32, smallest / len(cuts), top_value / len(cuts)))
        gain = gain * jnp.repeat(steps, extent[position] // shards_of).reshape([-1 if axis == position else 1 for axis in range(len(extent))])
    return gain


def noise(key, extent, width, most, pieces=(), kind=jnp.bfloat16):
    drawn = width * jax.random.normal(key, extent, jnp.float32)
    if pieces:
        drawn = drawn * block_scale(key, extent, pieces, -0.22, 0.18)
    return jnp.clip(drawn, -most, most).astype(kind)


def setup_inputs(seed: int = 0) -> dict:
    arg_keys = jax.random.split(jax.random.key(seed), 6)
    return {
        "leaf_mult": noise(arg_keys[0], (LEAVES, K), 1.0, 6.0, ((0, 32),), jnp.float32),
        "m2m_ops": noise(arg_keys[1], (8, K, K), (8 * K) ** -0.5, 0.125, (), jnp.float32),
        "m2l_ops": noise(arg_keys[2], (SLOTS, K, K), (SLOTS * K) ** -0.5, 0.0625, (), jnp.float32),
        "owner_box": draw_owner_box(jax.random.fold_in(arg_keys[5], 71), 0),
        "src_list": draw_src_list(jax.random.fold_in(arg_keys[5], 71), 0),
    }


def reference(leaf_mult, m2m_ops, m2l_ops, owner_box, src_list):
    children = leaf_mult.reshape(PARENTS, 8, K)
    parent_mult = jnp.einsum('pck,ckl->pl', children, m2m_ops, precision=lax.Precision.HIGHEST)
    owned_mult = jnp.take(parent_mult, owner_box, axis=0)
    present = src_list >= 0
    clamped = jnp.where(present, src_list, 0)

    def translate(args):
        slot_rows, slot_live = args
        sources = jnp.take(parent_mult, slot_rows, axis=0)
        sources = jnp.where(slot_live[:, :, None], sources, jnp.float32(0.0))
        return jnp.einsum('rjk,jkl->rl', sources, m2l_ops, precision=lax.Precision.HIGHEST)

    blocks = lax.map(translate, (clamped.reshape(N_SEG, GROUP, SLOTS), present.reshape(N_SEG, GROUP, SLOTS)))
    local_exp = blocks.reshape(PARENTS, K)
    return parent_mult, owned_mult, local_exp
```

```python
import functools

import jax
import jax.numpy as jnp
from jax import lax
from jax.experimental import pallas as pl
from jax.experimental.pallas import tpu as pltpu
from jax.sharding import PartitionSpec as P

MESH = pl.DeviceIdType.MESH
LANES = 128
BATCH = 4
PARTS = 4
EXCHANGE_VMEM = 24 << 20
COMBINE_VMEM = 16 << 20


def split(value):
    high = value.astype(jnp.bfloat16)
    low = (value - high.astype(jnp.float32)).astype(jnp.bfloat16)
    return high, low


def exchange(
    n_seg, n_sub, leaf_hbm, up_hbm, ops_hbm, box, ops_high, ops_low,
    leaf, up, ops, ops_sem, leaf_sem, up_sem, send_sem, recv_sem,
):
    seg, sub = lax.axis_index("seg"), lax.axis_index("sub")
    n_up, width = up.shape[0], up.shape[2]
    slots = ops.shape[0]
    rows = leaf.shape[1] // n_up
    n_high = n_sub // 2
    side, core, high = seg % 2, sub % 2, sub // 2
    partner = seg + 1 - 2 * side
    other_side = 1 - side
    sibling = sub + 1 - 2 * core
    target = seg + 2 - 4 * side
    origin = seg - 2 + 4 * side
    has_target = (target >= 0) & (target < n_seg)
    has_origin = (origin >= 0) & (origin < n_seg)
    tiles = width // LANES
    half = rows // PARTS
    group_rows = rows * n_sub
    empty_row = 3 * group_rows

    leaf_copies = [
        pltpu.make_async_copy(leaf_hbm.at[:, pl.ds(t * LANES, LANES)], leaf.at[t], leaf_sem.at[t])
        for t in range(tiles)
    ]
    for c in leaf_copies:
        c.start()
    up_copies = [pltpu.make_async_copy(up_hbm.at[c], up.at[c], up_sem.at[c]) for c in range(n_up)]
    for c in up_copies:
        c.start()
    middle = slots // 2
    ops_copies = [
        pltpu.make_async_copy(ops_hbm.at[at], ops.at[at], ops_sem.at[k])
        for k, at in enumerate((pl.ds(0, middle), pl.ds(middle, slots - middle)))
    ]

    barrier = pltpu.get_barrier_semaphore()

    def greet(to_seg, to_sub):
        pl.semaphore_signal(barrier, inc=1, device_id=(to_seg, to_sub), device_id_type=MESH)

    def peer(step):
        return lax.rem(high + step, n_high) * 2 + core

    greet(seg, sibling)
    greet(partner, sub)
    for step in range(1, n_high):
        greet(seg, peer(step))

    @pl.when(has_target)
    def _():
        greet(target, sub)

    @pl.when(has_origin)
    def _():
        greet(origin, sub)

    box[pl.ds(empty_row * tiles, 8 * tiles), :] = jnp.zeros((8 * tiles, LANES), jnp.float32)

    for c in leaf_copies:
        c.wait()
    total = jnp.zeros((rows, width), jnp.float32)
    for c in range(n_up):
        up_copies[c].wait()
        if c == n_up // 2:
            for one in ops_copies:
                one.start()
        child = jnp.concatenate(
            [leaf[t, pl.ds(c, rows, stride=n_up), :] for t in range(tiles)], axis=1
        )
        first, second = split(child)
        up_first, up_second = split(up[c])
        both = jnp.concatenate([first, second], axis=0)
        out = jnp.dot(both, up_first, preferred_element_type=jnp.float32)
        total = total + (out[:rows] + out[rows:])
        total = total + jnp.dot(first, up_second, preferred_element_type=jnp.float32)
    own_start = pl.multiple_of((side * n_sub + sub) * rows * tiles, 8)
    for t in range(tiles):
        box[pl.ds(own_start + t, rows, stride=tiles), :] = total[:, t * LANES : (t + 1) * LANES]

    pl.semaphore_wait(barrier, 1 + n_high + has_target.astype(jnp.int32) + has_origin.astype(jnp.int32))

    names = {}

    def copy(name, src, dst, to_seg, to_sub):
        k = names.setdefault(name, len(names))
        return pltpu.make_async_remote_copy(
            src_ref=src, dst_ref=dst, send_sem=send_sem.at[k], recv_sem=recv_sem.at[k],
            device_id=(to_seg, to_sub), device_id_type=MESH,
        )

    def place(group, k, part=None):
        start = (group * n_sub + k) * rows * tiles
        if part is None:
            return box.at[pl.ds(pl.multiple_of(start, 8), rows * tiles)]
        return box.at[pl.ds(pl.multiple_of(start + part * half * tiles, 8), half * tiles)]

    sent = []

    def go(c):
        c.start()
        sent.append(c)
        return c

    def to_x(part):
        at = place(side, sub, part)
        return copy(("x", part), at, at, partner, sub)

    def from_x(part):
        at = place(other_side, sub, part)
        return copy(("x", part), at, at, partner, sub)

    def to_y(step, part):
        at = place(side, sub, part)
        return copy(("y", step, part), at, at, seg, peer(step))

    def from_y(step, part):
        at = place(side, peer(n_high - step), part)
        return copy(("y", step, part), at, at, seg, peer(step))

    def xy(step, part):
        at = place(other_side, sub, part)
        return copy(("xy", step, part), at, at, seg, peer(step))

    def from_xy(step, part):
        at = place(other_side, peer(n_high - step), part)
        return copy(("xy", step, part), at, at, seg, peer(step))

    def yx(step, part):
        at = place(side, peer(step), part)
        return copy(("yx", step, part), at, at, partner, sub)

    def from_yx(step, part):
        at = place(other_side, peer(step), part)
        return copy(("yx", step, part), at, at, partner, sub)

    def z(step, part):
        return copy(
            ("z", step, part), place(other_side, peer(step), part), place(2, peer(step), part), target, sub
        )

    def to_sibling(step, which):
        at = place((side, other_side, 2)[which], peer(step))
        return copy(("s", step, which), at, at, seg, sibling)

    def from_sibling(step, which):
        s = lax.rem(high + step, n_high) * 2 + 1 - core
        at = place((side, other_side, 2)[which], s)
        return copy(("s", step, which), at, at, seg, sibling)

    for part in range(PARTS):
        go(to_x(part))
        for step in range(1, n_high):
            go(to_y(step, PARTS - 1 - part))
    go(to_sibling(0, 0))

    def split_ops(start, stop):
        @pl.loop(start, stop)
        def _(j):
            ops_high[j], ops_low[j] = split(ops[j])

    ops_copies[0].wait()
    split_ops(0, middle)

    for part in range(PARTS):
        from_x(part).wait_recv()

        @pl.when(has_target)
        def _():
            z(0, part).start()

        for step in range(1, n_high):
            if part < PARTS // 2:
                go(xy(step, part))
        for step in range(1, n_high):
            from_y(step, PARTS - 1 - part).wait_recv()
            if part < PARTS // 2:
                go(yx(n_high - step, PARTS - 1 - part))

    go(to_sibling(0, 1))
    for step in range(1, n_high):
        go(to_sibling(n_high - step, 0))

    for part in range(PARTS // 2):
        for step in range(1, n_high):
            from_xy(step, part).wait_recv()

            @pl.when(has_target)
            def _():
                z(n_high - step, part).start()

            from_yx(step, PARTS - 1 - part).wait_recv()

            @pl.when(has_target)
            def _():
                z(step, PARTS - 1 - part).start()

    for step in range(1, n_high):
        go(to_sibling(step, 1))

    ops_copies[1].wait()
    split_ops(middle, slots)

    for step in range(n_high):
        from_sibling(step, 0).wait_recv()

    for step in range(n_high):
        from_sibling(step, 1).wait_recv()

    @pl.when(has_origin)
    def _():
        for step in range(n_high):
            for part in range(PARTS):
                z(step, part).wait_recv()
            to_sibling(step, 2).start()
        for step in range(n_high):
            from_sibling(step, 2).wait_recv()

    for c in sent:
        c.wait_send()

    @pl.when(has_target)
    def _():
        for step in range(n_high):
            for part in range(PARTS):
                z(step, part).wait_send()

    @pl.when(has_origin)
    def _():
        for step in range(n_high):
            to_sibling(step, 2).wait_send()


def combine(
    n_sub, src_t, owner, box, ops_high, ops_low, parent_out, owned_out, local_out,
    where_v, where_s, first_rows, second_rows, where_sem,
):
    seg, sub = lax.axis_index("seg"), lax.axis_index("sub")
    rows, width = local_out.shape
    slots = src_t.shape[0]
    tiles = width // LANES
    side = seg % 2
    group_rows = rows * n_sub
    empty_row = 3 * group_rows
    batches = slots // BATCH

    pair_start = (seg - side) * group_rows
    table = jnp.concatenate([src_t[...], jnp.broadcast_to(owner[...], (8, rows))], axis=0)
    local = table - pair_start
    local = jnp.where(local < 0, local + 3 * group_rows, local)
    local = jnp.where(table < 0, empty_row, jnp.clip(local, 0, empty_row))
    where_v[...] = local * tiles
    where_copy = pltpu.make_async_copy(where_v, where_s, where_sem.at[0])
    where_copy.start()

    def spread(ref, start):
        return jnp.concatenate(
            [ref[pl.ds(start + t, rows, stride=tiles), :] for t in range(tiles)], axis=1
        )

    def gather(into, slot, count):
        for i in range(count):
            for r in range(rows):
                at = pl.ds(pl.multiple_of(where_s[slot + i, r], tiles), tiles)
                into[pl.ds((i * rows + r) * tiles, tiles), :] = box[at, :]

    parent_out[...] = spread(box, pl.multiple_of((side * n_sub + sub) * rows * tiles, 8))
    where_copy.wait()
    gather(second_rows, slots, 1)
    owned_out[...] = spread(second_rows, 0)
    gather(first_rows, 0, BATCH)
    local_out[...] = jnp.zeros((rows, width), jnp.float32)

    def translate(rows_of, slot):
        parts = [split(spread(rows_of, i * rows * tiles)) for i in range(BATCH)]
        first = jnp.concatenate([p[0] for p in parts], axis=1)
        second = jnp.concatenate([p[1] for p in parts], axis=1)
        both = jnp.concatenate([first, second], axis=0)
        ops_first = ops_high[pl.ds(slot, BATCH)].reshape(BATCH * width, width)
        ops_second = ops_low[pl.ds(slot, BATCH)].reshape(BATCH * width, width)
        out = jnp.dot(both, ops_first, preferred_element_type=jnp.float32)
        rest = jnp.dot(first, ops_second, preferred_element_type=jnp.float32)
        local_out[...] += out[:rows] + (out[rows:] + rest)

    @pl.loop(0, batches // 2 - 1)
    def _(b):
        slot = b * (2 * BATCH)
        gather(second_rows, slot + BATCH, BATCH)
        translate(first_rows, slot)
        gather(first_rows, slot + 2 * BATCH, BATCH)
        translate(second_rows, slot + BATCH)

    gather(second_rows, slots - BATCH, BATCH)
    translate(first_rows, slots - 2 * BATCH)
    translate(second_rows, slots - BATCH)


def on_device(n_seg, n_sub, leaf_mult, m2m_ops, m2l_ops, owner_box, src_list):
    rows, width = leaf_mult.shape[0] // 8, leaf_mult.shape[1]
    slots = src_list.shape[1]
    n_high = n_sub // 2
    messages = PARTS * (3 * n_high - 1) + 3 * n_high
    group_rows = rows * n_sub
    tiles = width // LANES
    vmem = pl.BlockSpec(memory_space=pltpu.VMEM)
    hbm = pl.BlockSpec(memory_space=pl.ANY)
    half_ops = jax.ShapeDtypeStruct(m2l_ops.shape, jnp.bfloat16)
    box, ops_high, ops_low = pl.pallas_call(
        functools.partial(exchange, n_seg, n_sub),
        out_shape=(
            jax.ShapeDtypeStruct(((3 * group_rows + 8) * tiles, LANES), jnp.float32), half_ops, half_ops
        ),
        in_specs=[hbm, hbm, hbm],
        out_specs=(vmem, vmem, vmem),
        scratch_shapes=[
            pltpu.VMEM((tiles, leaf_mult.shape[0], LANES), jnp.float32),
            pltpu.VMEM(m2m_ops.shape, jnp.float32),
            pltpu.VMEM(m2l_ops.shape, jnp.float32),
            pltpu.SemaphoreType.DMA((2,)),
            pltpu.SemaphoreType.DMA((tiles,)),
            pltpu.SemaphoreType.DMA((m2m_ops.shape[0],)),
            pltpu.SemaphoreType.DMA((messages,)),
            pltpu.SemaphoreType.DMA((messages,)),
        ],
        compiler_params=pltpu.CompilerParams(
            collective_id=0, has_side_effects=True, vmem_limit_bytes=EXCHANGE_VMEM
        ),
    )(*(pltpu.with_memory_space_constraint(a, pltpu.HBM) for a in (leaf_mult, m2m_ops, m2l_ops)))
    out = jax.ShapeDtypeStruct((rows, width), jnp.float32)
    return pl.pallas_call(
        functools.partial(combine, n_sub),
        out_shape=(out, out, out),
        in_specs=[vmem] * 5,
        out_specs=(vmem, vmem, vmem),
        scratch_shapes=[
            pltpu.VMEM((slots + 8, rows), jnp.int32),
            pltpu.SMEM((slots + 8, rows), jnp.int32),
            pltpu.VMEM((BATCH * rows * tiles, LANES), jnp.float32),
            pltpu.VMEM((BATCH * rows * tiles, LANES), jnp.float32),
            pltpu.SemaphoreType.DMA((1,)),
        ],
        compiler_params=pltpu.CompilerParams(vmem_limit_bytes=COMBINE_VMEM),
    )(src_list.T, owner_box.reshape(1, rows), box, ops_high, ops_low)


def solution(mesh):
    n_seg, n_sub = mesh.shape["seg"], mesh.shape["sub"]
    in_specs = (P(("seg", "sub"), None), P(), P(), P(("seg", "sub")), P(("seg", "sub"), None))
    out_specs = (P(("seg", "sub"), None), P(("seg", "sub"), None), P(("seg", "sub"), None))
    return jax.shard_map(
        functools.partial(on_device, n_seg, n_sub),
        mesh=mesh, in_specs=in_specs, out_specs=out_specs, check_vma=False,
    )
```

```python
import functools

import jax
import jax.numpy as jnp
from jax import lax
from jax.experimental import pallas as pl
from jax.experimental.pallas import tpu as pltpu
from jax.sharding import PartitionSpec as P

MESH = pl.DeviceIdType.MESH
LANES = 128
BATCH = 4
PARTS = 4
EXCHANGE_VMEM = 24 << 20
COMBINE_VMEM = 16 << 20


def split(value):
    high = value.astype(jnp.bfloat16)
    low = (value - high.astype(jnp.float32)).astype(jnp.bfloat16)
    return high, low


def exchange(
    n_seg, n_sub, leaf_hbm, up_hbm, ops_hbm, box, ops_high, ops_low,
    leaf, up, ops, ops_sem, leaf_sem, up_sem, send_sem, recv_sem,
):
    seg, sub = lax.axis_index("seg"), lax.axis_index("sub")
    n_up, width = up.shape[0], up.shape[2]
    slots = ops.shape[0]
    rows = leaf.shape[1] // n_up
    n_high = n_sub // 2
    side, core, high = seg % 2, sub % 2, sub // 2
    partner = seg + 1 - 2 * side
    other_side = 1 - side
    sibling = sub + 1 - 2 * core
    target = seg + 2 - 4 * side
    origin = seg - 2 + 4 * side
    has_target = (target >= 0) & (target < n_seg)
    has_origin = (origin >= 0) & (origin < n_seg)
    tiles = width // LANES
    half = rows // PARTS
    group_rows = rows * n_sub
    empty_row = 3 * group_rows

    leaf_copies = [
        pltpu.make_async_copy(leaf_hbm.at[:, pl.ds(t * LANES, LANES)], leaf.at[t], leaf_sem.at[t])
        for t in range(tiles)
    ]
    for c in leaf_copies:
        c.start()
    up_copies = [pltpu.make_async_copy(up_hbm.at[c], up.at[c], up_sem.at[c]) for c in range(n_up)]
    for c in up_copies:
        c.start()
    middle = slots // 2
    ops_copies = [
        pltpu.make_async_copy(ops_hbm.at[at], ops.at[at], ops_sem.at[k])
        for k, at in enumerate((pl.ds(0, middle), pl.ds(middle, slots - middle)))
    ]

    barrier = pltpu.get_barrier_semaphore()

    def greet(to_seg, to_sub):
        pl.semaphore_signal(barrier, inc=1, device_id=(to_seg, to_sub), device_id_type=MESH)

    def peer(step):
        return lax.rem(high + step, n_high) * 2 + core

    greet(seg, sibling)
    greet(partner, sub)
    for step in range(1, n_high):
        greet(seg, peer(step))

    @pl.when(has_target)
    def _():
        greet(target, sub)

    @pl.when(has_origin)
    def _():
        greet(origin, sub)

    box[pl.ds(empty_row * tiles, 8 * tiles), :] = jnp.zeros((8 * tiles, LANES), jnp.float32)

    for c in leaf_copies:
        c.wait()
    total = jnp.zeros((rows, width), jnp.float32)
    for c in range(n_up):
        up_copies[c].wait()
        if c == n_up // 2:
            for one in ops_copies:
                one.start()
        child = jnp.concatenate(
            [leaf[t, pl.ds(c, rows, stride=n_up), :] for t in range(tiles)], axis=1
        )
        first, second = split(child)
        up_first, up_second = split(up[c])
        both = jnp.concatenate([first, second], axis=0)
        out = jnp.dot(both, up_first, preferred_element_type=jnp.float32)
        total = total + (out[:rows] + out[rows:])
        total = total + jnp.dot(first, up_second, preferred_element_type=jnp.float32)
    own_start = pl.multiple_of((side * n_sub + sub) * rows * tiles, 8)
    for t in range(tiles):
        box[pl.ds(own_start + t, rows, stride=tiles), :] = total[:, t * LANES : (t + 1) * LANES]

    pl.semaphore_wait(barrier, 1 + n_high + has_target.astype(jnp.int32) + has_origin.astype(jnp.int32))

    names = {}

    def copy(name, src, dst, to_seg, to_sub):
        k = names.setdefault(name, len(names))
        return pltpu.make_async_remote_copy(
            src_ref=src, dst_ref=dst, send_sem=send_sem.at[k], recv_sem=recv_sem.at[k],
            device_id=(to_seg, to_sub), device_id_type=MESH,
        )

    def place(group, k, part=None):
        start = (group * n_sub + k) * rows * tiles
        if part is None:
            return box.at[pl.ds(pl.multiple_of(start, 8), rows * tiles)]
        return box.at[pl.ds(pl.multiple_of(start + part * half * tiles, 8), half * tiles)]

    sent = []

    def go(c):
        c.start()
        sent.append(c)
        return c

    def to_x(part):
        at = place(side, sub, part)
        return copy(("x", part), at, at, partner, sub)

    def from_x(part):
        at = place(other_side, sub, part)
        return copy(("x", part), at, at, partner, sub)

    def to_y(step, part):
        at = place(side, sub, part)
        return copy(("y", step, part), at, at, seg, peer(step))

    def from_y(step, part):
        at = place(side, peer(n_high - step), part)
        return copy(("y", step, part), at, at, seg, peer(step))

    def xy(step, part):
        at = place(other_side, sub, part)
        return copy(("xy", step, part), at, at, seg, peer(step))

    def from_xy(step, part):
        at = place(other_side, peer(n_high - step), part)
        return copy(("xy", step, part), at, at, seg, peer(step))

    def yx(step, part):
        at = place(side, peer(step), part)
        return copy(("yx", step, part), at, at, partner, sub)

    def from_yx(step, part):
        at = place(other_side, peer(step), part)
        return copy(("yx", step, part), at, at, partner, sub)

    def z(step, part):
        return copy(
            ("z", step, part), place(other_side, peer(step), part), place(2, peer(step), part), target, sub
        )

    def to_sibling(step, which):
        at = place((side, other_side, 2)[which], peer(step))
        return copy(("s", step, which), at, at, seg, sibling)

    def from_sibling(step, which):
        s = lax.rem(high + step, n_high) * 2 + 1 - core
        at = place((side, other_side, 2)[which], s)
        return copy(("s", step, which), at, at, seg, sibling)

    for part in range(PARTS):
        go(to_x(part))
        for step in range(1, n_high):
            go(to_y(step, PARTS - 1 - part))
    go(to_sibling(0, 0))

    def split_ops(start, stop):
        @pl.loop(start, stop)
        def _(j):
            ops_high[j], ops_low[j] = split(ops[j])

    ops_copies[0].wait()
    split_ops(0, middle)

    for part in range(PARTS):
        from_x(part).wait_recv()

        @pl.when(has_target)
        def _():
            z(0, part).start()

        for step in range(1, n_high):
            if part < PARTS // 2:
                go(xy(step, part))
        for step in range(1, n_high):
            from_y(step, PARTS - 1 - part).wait_recv()
            if part < PARTS // 2:
                go(yx(n_high - step, PARTS - 1 - part))

    go(to_sibling(0, 1))
    for step in range(1, n_high):
        go(to_sibling(n_high - step, 0))

    for part in range(PARTS // 2):
        for step in range(1, n_high):
            from_xy(step, part).wait_recv()

            @pl.when(has_target)
            def _():
                z(n_high - step, part).start()

            from_yx(step, PARTS - 1 - part).wait_recv()

            @pl.when(has_target)
            def _():
                z(step, PARTS - 1 - part).start()

    for step in range(1, n_high):
        go(to_sibling(step, 1))

    ops_copies[1].wait()
    split_ops(middle, slots)

    for step in range(n_high):
        from_sibling(step, 0).wait_recv()

    for step in range(n_high):
        from_sibling(step, 1).wait_recv()

    @pl.when(has_origin)
    def _():
        for step in range(n_high):
            for part in range(PARTS):
                z(step, part).wait_recv()
            to_sibling(step, 2).start()
        for step in range(n_high):
            from_sibling(step, 2).wait_recv()

    for c in sent:
        c.wait_send()

    @pl.when(has_target)
    def _():
        for step in range(n_high):
            for part in range(PARTS):
                z(step, part).wait_send()

    @pl.when(has_origin)
    def _():
        for step in range(n_high):
            to_sibling(step, 2).wait_send()


def combine(
    n_sub, src_t, owner, box, ops_high, ops_low, parent_out, owned_out, local_out,
    where_v, where_s, first_rows, second_rows, where_sem,
):
    seg, sub = lax.axis_index("seg"), lax.axis_index("sub")
    rows, width = local_out.shape
    slots = src_t.shape[0]
    tiles = width // LANES
    side = seg % 2
    group_rows = rows * n_sub
    empty_row = 3 * group_rows
    batches = slots // BATCH

    pair_start = (seg - side) * group_rows
    table = jnp.concatenate([src_t[...], jnp.broadcast_to(owner[...], (8, rows))], axis=0)
    local = table - pair_start
    local = jnp.where(local < 0, local + 3 * group_rows, local)
    local = jnp.where(table < 0, empty_row, jnp.clip(local, 0, empty_row))
    where_v[...] = local * tiles
    where_copy = pltpu.make_async_copy(where_v, where_s, where_sem.at[0])
    where_copy.start()

    def spread(ref, start):
        return jnp.concatenate(
            [ref[pl.ds(start + t, rows, stride=tiles), :] for t in range(tiles)], axis=1
        )

    def gather(into, slot, count):
        for i in range(count):
            for r in range(rows):
                at = pl.ds(pl.multiple_of(where_s[slot + i, r], tiles), tiles)
                into[pl.ds((i * rows + r) * tiles, tiles), :] = box[at, :]

    parent_out[...] = spread(box, pl.multiple_of((side * n_sub + sub) * rows * tiles, 8))
    where_copy.wait()
    gather(second_rows, slots, 1)
    owned_out[...] = spread(second_rows, 0)
    gather(first_rows, 0, BATCH)
    local_out[...] = jnp.zeros((rows, width), jnp.float32)

    def translate(rows_of, slot):
        parts = [split(spread(rows_of, i * rows * tiles)) for i in range(BATCH)]
        first = jnp.concatenate([p[0] for p in parts], axis=1)
        second = jnp.concatenate([p[1] for p in parts], axis=1)
        both = jnp.concatenate([first, second], axis=0)
        ops_first = ops_high[pl.ds(slot, BATCH)].reshape(BATCH * width, width)
        ops_second = ops_low[pl.ds(slot, BATCH)].reshape(BATCH * width, width)
        out = jnp.dot(both, ops_first, preferred_element_type=jnp.float32)
        rest = jnp.dot(first, ops_second, preferred_element_type=jnp.float32)
        local_out[...] += out[:rows] + (out[rows:] + rest)

    for b in range(0, batches, 2):
        slot = b * BATCH
        gather(second_rows, slot + BATCH, BATCH)
        translate(first_rows, slot)
        if b + 2 < batches:
            gather(first_rows, slot + 2 * BATCH, BATCH)
        translate(second_rows, slot + BATCH)


def on_device(n_seg, n_sub, leaf_mult, m2m_ops, m2l_ops, owner_box, src_list):
    rows, width = leaf_mult.shape[0] // 8, leaf_mult.shape[1]
    slots = src_list.shape[1]
    n_high = n_sub // 2
    messages = PARTS * (3 * n_high - 1) + 3 * n_high
    group_rows = rows * n_sub
    tiles = width // LANES
    vmem = pl.BlockSpec(memory_space=pltpu.VMEM)
    hbm = pl.BlockSpec(memory_space=pl.ANY)
    half_ops = jax.ShapeDtypeStruct(m2l_ops.shape, jnp.bfloat16)
    box, ops_high, ops_low = pl.pallas_call(
        functools.partial(exchange, n_seg, n_sub),
        out_shape=(
            jax.ShapeDtypeStruct(((3 * group_rows + 8) * tiles, LANES), jnp.float32), half_ops, half_ops
        ),
        in_specs=[hbm, hbm, hbm],
        out_specs=(vmem, vmem, vmem),
        scratch_shapes=[
            pltpu.VMEM((tiles, leaf_mult.shape[0], LANES), jnp.float32),
            pltpu.VMEM(m2m_ops.shape, jnp.float32),
            pltpu.VMEM(m2l_ops.shape, jnp.float32),
            pltpu.SemaphoreType.DMA((2,)),
            pltpu.SemaphoreType.DMA((tiles,)),
            pltpu.SemaphoreType.DMA((m2m_ops.shape[0],)),
            pltpu.SemaphoreType.DMA((messages,)),
            pltpu.SemaphoreType.DMA((messages,)),
        ],
        compiler_params=pltpu.CompilerParams(
            collective_id=0, has_side_effects=True, vmem_limit_bytes=EXCHANGE_VMEM
        ),
    )(*(pltpu.with_memory_space_constraint(a, pltpu.HBM) for a in (leaf_mult, m2m_ops, m2l_ops)))
    out = jax.ShapeDtypeStruct((rows, width), jnp.float32)
    return pl.pallas_call(
        functools.partial(combine, n_sub),
        out_shape=(out, out, out),
        in_specs=[vmem] * 5,
        out_specs=(vmem, vmem, vmem),
        scratch_shapes=[
            pltpu.VMEM((slots + 8, rows), jnp.int32),
            pltpu.SMEM((slots + 8, rows), jnp.int32),
            pltpu.VMEM((BATCH * rows * tiles, LANES), jnp.float32),
            pltpu.VMEM((BATCH * rows * tiles, LANES), jnp.float32),
            pltpu.SemaphoreType.DMA((1,)),
        ],
        compiler_params=pltpu.CompilerParams(vmem_limit_bytes=COMBINE_VMEM),
    )(src_list.T, owner_box.reshape(1, rows), box, ops_high, ops_low)


def solution(mesh):
    n_seg, n_sub = mesh.shape["seg"], mesh.shape["sub"]
    in_specs = (P(("seg", "sub"), None), P(), P(), P(("seg", "sub")), P(("seg", "sub"), None))
    out_specs = (P(("seg", "sub"), None), P(("seg", "sub"), None), P(("seg", "sub"), None))
    return jax.shard_map(
        functools.partial(on_device, n_seg, n_sub),
        mesh=mesh, in_specs=in_specs, out_specs=out_specs, check_vma=False,
    )
```

```python
import functools

import jax
import jax.numpy as jnp
from jax import lax
from jax.experimental import pallas as pl
from jax.experimental.pallas import tpu as pltpu
from jax.sharding import PartitionSpec as P

MESH = pl.DeviceIdType.MESH
LANES = 128
BATCH = 4
PARTS = 4
DIRECT = 1
CROSS = 1
EXCHANGE_VMEM = 24 << 20
COMBINE_VMEM = 16 << 20


def split(value):
    high = value.astype(jnp.bfloat16)
    low = (value - high.astype(jnp.float32)).astype(jnp.bfloat16)
    return high, low


def exchange(
    n_seg, n_sub, leaf_hbm, up_hbm, ops_hbm, box, ops_high, ops_low,
    leaf, up, ops, relay, ops_sem, leaf_sem, up_sem, send_sem, recv_sem,
):
    seg, sub = lax.axis_index("seg"), lax.axis_index("sub")
    n_up, width = up.shape[0], up.shape[2]
    slots = ops.shape[0]
    rows = leaf.shape[1] // n_up
    n_high = n_sub // 2
    side, core, high = seg % 2, sub % 2, sub // 2
    partner = seg + 1 - 2 * side
    other_side = 1 - side
    sibling = sub + 1 - 2 * core
    target = seg + 2 - 4 * side
    origin = seg - 2 + 4 * side
    has_target = (target >= 0) & (target < n_seg)
    has_origin = (origin >= 0) & (origin < n_seg)
    tiles = width // LANES
    half = rows // PARTS
    group_rows = rows * n_sub
    empty_row = 3 * group_rows

    leaf_copies = [
        pltpu.make_async_copy(leaf_hbm.at[:, pl.ds(t * LANES, LANES)], leaf.at[t], leaf_sem.at[t])
        for t in range(tiles)
    ]
    for c in leaf_copies:
        c.start()
    up_copies = [pltpu.make_async_copy(up_hbm.at[c], up.at[c], up_sem.at[c]) for c in range(n_up)]
    for c in up_copies:
        c.start()
    middle = slots // 2
    ops_copies = [
        pltpu.make_async_copy(ops_hbm.at[at], ops.at[at], ops_sem.at[k])
        for k, at in enumerate((pl.ds(0, middle), pl.ds(middle, slots - middle)))
    ]

    barrier = pltpu.get_barrier_semaphore()

    def greet(to_seg, to_sub):
        pl.semaphore_signal(barrier, inc=1, device_id=(to_seg, to_sub), device_id_type=MESH)

    def peer(step):
        return lax.rem(high + step, n_high) * 2 + core

    greet(seg, sibling)
    greet(partner, sub)
    for step in range(1, n_high):
        greet(seg, peer(step))

    @pl.when(has_target)
    def _():
        greet(target, sub)
        for step in range(1, n_high):
            greet(target, peer(step))

    @pl.when(has_origin)
    def _():
        greet(origin, sub)
        for step in range(1, n_high):
            greet(origin, peer(step))

    box[pl.ds(empty_row * tiles, 8 * tiles), :] = jnp.zeros((8 * tiles, LANES), jnp.float32)

    for c in leaf_copies:
        c.wait()
    total = jnp.zeros((rows, width), jnp.float32)
    for c in range(n_up):
        up_copies[c].wait()
        if c == n_up // 2:
            for one in ops_copies:
                one.start()
        child = jnp.concatenate(
            [leaf[t, pl.ds(c, rows, stride=n_up), :] for t in range(tiles)], axis=1
        )
        first, second = split(child)
        up_first, up_second = split(up[c])
        both = jnp.concatenate([first, second], axis=0)
        out = jnp.dot(both, up_first, preferred_element_type=jnp.float32)
        total = total + (out[:rows] + out[rows:])
        total = total + jnp.dot(first, up_second, preferred_element_type=jnp.float32)
    own_start = pl.multiple_of((side * n_sub + sub) * rows * tiles, 8)
    for t in range(tiles):
        box[pl.ds(own_start + t, rows, stride=tiles), :] = total[:, t * LANES : (t + 1) * LANES]

    pl.semaphore_wait(
        barrier, 1 + n_high + n_high * (has_target.astype(jnp.int32) + has_origin.astype(jnp.int32))
    )

    names = {}

    def copy(name, src, dst, to_seg, to_sub):
        k = names.setdefault(name, len(names))
        return pltpu.make_async_remote_copy(
            src_ref=src, dst_ref=dst, send_sem=send_sem.at[k], recv_sem=recv_sem.at[k],
            device_id=(to_seg, to_sub), device_id_type=MESH,
        )

    def place(group, k, part=None):
        start = (group * n_sub + k) * rows * tiles
        if part is None:
            return box.at[pl.ds(pl.multiple_of(start, 8), rows * tiles)]
        return box.at[pl.ds(pl.multiple_of(start + part * half * tiles, 8), half * tiles)]

    sent = []

    def go(c, when=None):
        sent.append((c, when))
        if when is None:
            c.start()
        else:
            pl.when(when)(c.start)

    def to_x(part):
        at = place(side, sub, part)
        return copy(("x", part), at, at, partner, sub)

    def from_x(part):
        at = place(other_side, sub, part)
        return copy(("x", part), at, at, partner, sub)

    def to_y(step, part):
        at = place(side, sub, part)
        return copy(("y", step, part), at, at, seg, peer(step))

    def from_y(step, part):
        at = place(side, peer(n_high - step), part)
        return copy(("y", step, part), at, at, seg, peer(step))

    def over_z(part):
        return copy(("o", part), place(side, sub, part), relay.at[part], origin, sub)

    def over_x(part):
        return copy(("ox", part), relay.at[part], place(2, sub, part), partner, sub)

    def xy(step, part):
        at = place(other_side, sub, part)
        return copy(("xy", step, part), at, at, seg, peer(step))

    def from_xy(step, part):
        at = place(other_side, peer(n_high - step), part)
        return copy(("xy", step, part), at, at, seg, peer(step))

    def yx(step, part):
        at = place(side, peer(step), part)
        return copy(("yx", step, part), at, at, partner, sub)

    def from_yx(step, part):
        at = place(other_side, peer(step), part)
        return copy(("yx", step, part), at, at, partner, sub)

    def z(part):
        return copy(("z", part), place(other_side, sub, part), place(2, sub, part), target, sub)

    def yz(step, part):
        return copy(
            ("yz", step, part), place(other_side, sub, part), place(2, sub, part), target, peer(step)
        )

    def from_yz(step, part):
        at = place(2, peer(n_high - step), part)
        return copy(("yz", step, part), at, at, target, peer(step))

    def to_sibling(group, step, part=None):
        at = place((side, other_side, 2)[group], peer(step), part)
        return copy(("s", group, step, part), at, at, seg, sibling)

    def from_sibling(group, step, part=None):
        theirs = lax.rem(high + step, n_high) * 2 + 1 - core
        at = place((side, other_side, 2)[group], theirs, part)
        return copy(("s", group, step, part), at, at, seg, sibling)

    parts = list(range(PARTS))
    through_x, through_z = parts[DIRECT:], parts[:DIRECT]
    y_order = parts[CROSS:] + parts[:CROSS]

    for i in parts:
        go(to_x(i))
        for step in range(1, n_high):
            go(to_y(step, y_order[i]))
        if i < len(through_x):
            go(over_z(through_x[i]), has_origin)
    go(to_sibling(0, 0))

    def split_ops(start, stop):
        @pl.loop(start, stop)
        def _(j):
            ops_high[j], ops_low[j] = split(ops[j])

    ops_copies[0].wait()
    split_ops(0, middle)

    for i in parts:
        from_x(i).wait_recv()
        for step in range(1, n_high):
            go(yz(step, i), has_target)
        if i in through_z:
            go(z(i), has_target)
        for step in range(1, n_high):
            if i < CROSS:
                go(xy(step, i))
        if i < len(through_x):
            pl.when(has_target)(over_z(through_x[i]).wait_recv)
            go(over_x(through_x[i]), has_target)
        for step in range(1, n_high):
            from_y(step, y_order[i]).wait_recv()
            if y_order[i] >= CROSS:
                go(yx(n_high - step, y_order[i]))

    go(to_sibling(1, 0))
    for step in range(1, n_high):
        go(to_sibling(0, n_high - step))

    ops_copies[1].wait()
    split_ops(middle, slots)

    for i in parts:
        one = z(i) if i in through_z else over_x(i)
        pl.when(has_origin)(one.wait_recv)
        go(to_sibling(2, 0, i), has_origin)
        for step in range(1, n_high):
            if i < CROSS:
                from_xy(step, i).wait_recv()
                go(to_sibling(1, n_high - step, i))
            else:
                from_yx(step, i).wait_recv()
                go(to_sibling(1, step, i))
            pl.when(has_origin)(from_yz(step, i).wait_recv)
            go(to_sibling(2, n_high - step, i), has_origin)

    for step in range(n_high):
        from_sibling(0, step).wait_recv()
    from_sibling(1, 0).wait_recv()
    for step in range(1, n_high):
        for i in parts:
            from_sibling(1, step, i).wait_recv()

    @pl.when(has_origin)
    def _():
        for step in range(n_high):
            for i in parts:
                from_sibling(2, step, i).wait_recv()

    for c, when in sent:
        if when is None:
            c.wait_send()
        else:
            pl.when(when)(c.wait_send)


def combine(
    n_sub, src_t, owner, box, ops_high, ops_low, parent_out, owned_out, local_out,
    where_v, where_s, first_rows, second_rows, where_sem,
):
    seg, sub = lax.axis_index("seg"), lax.axis_index("sub")
    rows, width = local_out.shape
    slots = src_t.shape[0]
    tiles = width // LANES
    side = seg % 2
    group_rows = rows * n_sub
    empty_row = 3 * group_rows
    batches = slots // BATCH

    pair_start = (seg - side) * group_rows
    table = jnp.concatenate([src_t[...], jnp.broadcast_to(owner[...], (8, rows))], axis=0)
    local = table - pair_start
    local = jnp.where(local < 0, local + 3 * group_rows, local)
    local = jnp.where(table < 0, empty_row, jnp.clip(local, 0, empty_row))
    where_v[...] = local * tiles
    where_copy = pltpu.make_async_copy(where_v, where_s, where_sem.at[0])
    where_copy.start()

    def spread(ref, start):
        return jnp.concatenate(
            [ref[pl.ds(start + t, rows, stride=tiles), :] for t in range(tiles)], axis=1
        )

    def gather(into, slot, count):
        for i in range(count):
            for r in range(rows):
                at = pl.ds(pl.multiple_of(where_s[slot + i, r], tiles), tiles)
                into[pl.ds((i * rows + r) * tiles, tiles), :] = box[at, :]

    parent_out[...] = spread(box, pl.multiple_of((side * n_sub + sub) * rows * tiles, 8))
    where_copy.wait()
    gather(second_rows, slots, 1)
    owned_out[...] = spread(second_rows, 0)
    gather(first_rows, 0, BATCH)
    local_out[...] = jnp.zeros((rows, width), jnp.float32)

    def translate(rows_of, slot):
        parts = [split(spread(rows_of, i * rows * tiles)) for i in range(BATCH)]
        first = jnp.concatenate([p[0] for p in parts], axis=1)
        second = jnp.concatenate([p[1] for p in parts], axis=1)
        both = jnp.concatenate([first, second], axis=0)
        ops_first = ops_high[pl.ds(slot, BATCH)].reshape(BATCH * width, width)
        ops_second = ops_low[pl.ds(slot, BATCH)].reshape(BATCH * width, width)
        out = jnp.dot(both, ops_first, preferred_element_type=jnp.float32)
        rest = jnp.dot(first, ops_second, preferred_element_type=jnp.float32)
        local_out[...] += out[:rows] + (out[rows:] + rest)

    for b in range(0, batches, 2):
        slot = b * BATCH
        gather(second_rows, slot + BATCH, BATCH)
        translate(first_rows, slot)
        if b + 2 < batches:
            gather(first_rows, slot + 2 * BATCH, BATCH)
        translate(second_rows, slot + BATCH)


def on_device(n_seg, n_sub, leaf_mult, m2m_ops, m2l_ops, owner_box, src_list):
    rows, width = leaf_mult.shape[0] // 8, leaf_mult.shape[1]
    slots = src_list.shape[1]
    n_high = n_sub // 2
    messages = PARTS * (4 + 5 * (n_high - 1)) + 1 + n_high
    group_rows = rows * n_sub
    tiles = width // LANES
    vmem = pl.BlockSpec(memory_space=pltpu.VMEM)
    hbm = pl.BlockSpec(memory_space=pl.ANY)
    half_ops = jax.ShapeDtypeStruct(m2l_ops.shape, jnp.bfloat16)
    box, ops_high, ops_low = pl.pallas_call(
        functools.partial(exchange, n_seg, n_sub),
        out_shape=(
            jax.ShapeDtypeStruct(((3 * group_rows + 8) * tiles, LANES), jnp.float32), half_ops, half_ops
        ),
        in_specs=[hbm, hbm, hbm],
        out_specs=(vmem, vmem, vmem),
        scratch_shapes=[
            pltpu.VMEM((tiles, leaf_mult.shape[0], LANES), jnp.float32),
            pltpu.VMEM(m2m_ops.shape, jnp.float32),
            pltpu.VMEM(m2l_ops.shape, jnp.float32),
            pltpu.VMEM((PARTS, rows // PARTS * tiles, LANES), jnp.float32),
            pltpu.SemaphoreType.DMA((2,)),
            pltpu.SemaphoreType.DMA((tiles,)),
            pltpu.SemaphoreType.DMA((m2m_ops.shape[0],)),
            pltpu.SemaphoreType.DMA((messages,)),
            pltpu.SemaphoreType.DMA((messages,)),
        ],
        compiler_params=pltpu.CompilerParams(
            collective_id=0, has_side_effects=True, vmem_limit_bytes=EXCHANGE_VMEM
        ),
    )(*(pltpu.with_memory_space_constraint(a, pltpu.HBM) for a in (leaf_mult, m2m_ops, m2l_ops)))
    out = jax.ShapeDtypeStruct((rows, width), jnp.float32)
    return pl.pallas_call(
        functools.partial(combine, n_sub),
        out_shape=(out, out, out),
        in_specs=[vmem] * 5,
        out_specs=(vmem, vmem, vmem),
        scratch_shapes=[
            pltpu.VMEM((slots + 8, rows), jnp.int32),
            pltpu.SMEM((slots + 8, rows), jnp.int32),
            pltpu.VMEM((BATCH * rows * tiles, LANES), jnp.float32),
            pltpu.VMEM((BATCH * rows * tiles, LANES), jnp.float32),
            pltpu.SemaphoreType.DMA((1,)),
        ],
        compiler_params=pltpu.CompilerParams(vmem_limit_bytes=COMBINE_VMEM),
    )(src_list.T, owner_box.reshape(1, rows), box, ops_high, ops_low)


def solution(mesh):
    n_seg, n_sub = mesh.shape["seg"], mesh.shape["sub"]
    in_specs = (P(("seg", "sub"), None), P(), P(), P(("seg", "sub")), P(("seg", "sub"), None))
    out_specs = (P(("seg", "sub"), None), P(("seg", "sub"), None), P(("seg", "sub"), None))
    return jax.shard_map(
        functools.partial(on_device, n_seg, n_sub),
        mesh=mesh, in_specs=in_specs, out_specs=out_specs, check_vma=False,
    )
```

```python
import functools

import jax
import jax.numpy as jnp
from jax import lax
from jax.experimental import pallas as pl
from jax.experimental.pallas import tpu as pltpu
from jax.sharding import PartitionSpec as P

MESH = pl.DeviceIdType.MESH
LANES = 128
BATCH = 4
PARTS = 4
DIRECT = 1
CROSS = 1
CHILDREN = 4
EXCHANGE_VMEM = 24 << 20
COMBINE_VMEM = 16 << 20


def split(value):
    high = value.astype(jnp.bfloat16)
    low = (value - high.astype(jnp.float32)).astype(jnp.bfloat16)
    return high, low


def exchange(
    n_seg, n_sub, leaf_hbm, up_hbm, ops_hbm, box, ops_high, ops_low,
    leaf, up, ops, relay, ops_sem, leaf_sem, up_sem, send_sem, recv_sem,
):
    seg, sub = lax.axis_index("seg"), lax.axis_index("sub")
    n_up, width = up.shape[0], up.shape[2]
    slots = ops.shape[0]
    rows = leaf.shape[1] // n_up
    n_high = n_sub // 2
    side, core, high = seg % 2, sub % 2, sub // 2
    partner = seg + 1 - 2 * side
    other_side = 1 - side
    sibling = sub + 1 - 2 * core
    target = seg + 2 - 4 * side
    origin = seg - 2 + 4 * side
    has_target = (target >= 0) & (target < n_seg)
    has_origin = (origin >= 0) & (origin < n_seg)
    tiles = width // LANES
    half = rows // PARTS
    group_rows = rows * n_sub
    empty_row = 3 * group_rows

    leaf_copies = [
        pltpu.make_async_copy(leaf_hbm.at[:, pl.ds(t * LANES, LANES)], leaf.at[t], leaf_sem.at[t])
        for t in range(tiles)
    ]
    for c in leaf_copies:
        c.start()
    middle = slots // 2
    ops_copies = [
        pltpu.make_async_copy(ops_hbm.at[at], ops.at[at], ops_sem.at[k])
        for k, at in enumerate((pl.ds(0, middle), pl.ds(middle, slots - middle)))
    ]

    barrier = pltpu.get_barrier_semaphore()

    def greet(to_seg, to_sub):
        pl.semaphore_signal(barrier, inc=1, device_id=(to_seg, to_sub), device_id_type=MESH)

    def peer(step):
        return lax.rem(high + step, n_high) * 2 + core

    greet(seg, sibling)
    greet(partner, sub)
    for step in range(1, n_high):
        greet(seg, peer(step))

    @pl.when(has_target)
    def _():
        greet(target, sub)
        for step in range(1, n_high):
            greet(target, peer(step))

    @pl.when(has_origin)
    def _():
        greet(origin, sub)
        for step in range(1, n_high):
            greet(origin, peer(step))

    up_copies = [
        pltpu.make_async_copy(
            up_hbm.at[pl.ds(c, CHILDREN)], up.at[pl.ds(c, CHILDREN)], up_sem.at[c // CHILDREN]
        )
        for c in range(0, n_up, CHILDREN)
    ]
    for c in up_copies:
        c.start()

    box[pl.ds(empty_row * tiles, 8 * tiles), :] = jnp.zeros((8 * tiles, LANES), jnp.float32)

    for c in leaf_copies:
        c.wait()
    total = None
    for k, one in enumerate(up_copies):
        one.wait()
        if k == len(up_copies) - 1:
            for c in ops_copies:
                c.start()
        child = jnp.concatenate(
            [
                leaf[t, pl.ds(k * CHILDREN + c, rows, stride=n_up), :]
                for c in range(CHILDREN) for t in range(tiles)
            ],
            axis=1,
        )
        first, second = split(child)
        up_first, up_second = split(up[pl.ds(k * CHILDREN, CHILDREN)].reshape(CHILDREN * width, width))
        both = jnp.concatenate([first, second], axis=0)
        out = jnp.dot(both, up_first, preferred_element_type=jnp.float32)
        rest = jnp.dot(first, up_second, preferred_element_type=jnp.float32)
        term = out[:rows] + (out[rows:] + rest)
        total = term if total is None else total + term
    own_start = pl.multiple_of((side * n_sub + sub) * rows * tiles, 8)
    for t in range(tiles):
        box[pl.ds(own_start + t, rows, stride=tiles), :] = total[:, t * LANES : (t + 1) * LANES]

    pl.semaphore_wait(
        barrier, 1 + n_high + n_high * (has_target.astype(jnp.int32) + has_origin.astype(jnp.int32))
    )

    names = {}

    def copy(name, src, dst, to_seg, to_sub):
        k = names.setdefault(name, len(names))
        return pltpu.make_async_remote_copy(
            src_ref=src, dst_ref=dst, send_sem=send_sem.at[k], recv_sem=recv_sem.at[k],
            device_id=(to_seg, to_sub), device_id_type=MESH,
        )

    def place(group, k, part=None):
        start = (group * n_sub + k) * rows * tiles
        if part is None:
            return box.at[pl.ds(pl.multiple_of(start, 8), rows * tiles)]
        return box.at[pl.ds(pl.multiple_of(start + part * half * tiles, 8), half * tiles)]

    sent = []

    def go(c, when=None):
        sent.append((c, when))
        if when is None:
            c.start()
        else:
            pl.when(when)(c.start)

    def to_x(part):
        at = place(side, sub, part)
        return copy(("x", part), at, at, partner, sub)

    def from_x(part):
        at = place(other_side, sub, part)
        return copy(("x", part), at, at, partner, sub)

    def to_y(step, part):
        at = place(side, sub, part)
        return copy(("y", step, part), at, at, seg, peer(step))

    def from_y(step, part):
        at = place(side, peer(n_high - step), part)
        return copy(("y", step, part), at, at, seg, peer(step))

    def over_z(part):
        return copy(("o", part), place(side, sub, part), relay.at[part], origin, sub)

    def over_x(part):
        return copy(("ox", part), relay.at[part], place(2, sub, part), partner, sub)

    def xy(step, part):
        at = place(other_side, sub, part)
        return copy(("xy", step, part), at, at, seg, peer(step))

    def from_xy(step, part):
        at = place(other_side, peer(n_high - step), part)
        return copy(("xy", step, part), at, at, seg, peer(step))

    def yx(step, part):
        at = place(side, peer(step), part)
        return copy(("yx", step, part), at, at, partner, sub)

    def from_yx(step, part):
        at = place(other_side, peer(step), part)
        return copy(("yx", step, part), at, at, partner, sub)

    def z(part):
        return copy(("z", part), place(other_side, sub, part), place(2, sub, part), target, sub)

    def yz(step, part):
        return copy(
            ("yz", step, part), place(other_side, sub, part), place(2, sub, part), target, peer(step)
        )

    def from_yz(step, part):
        at = place(2, peer(n_high - step), part)
        return copy(("yz", step, part), at, at, target, peer(step))

    def to_sibling(group, step, part=None):
        at = place((side, other_side, 2)[group], peer(step), part)
        return copy(("s", group, step, part), at, at, seg, sibling)

    def from_sibling(group, step, part=None):
        theirs = lax.rem(high + step, n_high) * 2 + 1 - core
        at = place((side, other_side, 2)[group], theirs, part)
        return copy(("s", group, step, part), at, at, seg, sibling)

    parts = list(range(PARTS))
    through_x, through_z = parts[DIRECT:], parts[:DIRECT]
    y_order = parts[CROSS:] + parts[:CROSS]

    for i in parts:
        go(to_x(i))
        for step in range(1, n_high):
            go(to_y(step, y_order[i]))
        if i < len(through_x):
            go(over_z(through_x[i]), has_origin)
    go(to_sibling(0, 0))

    def split_ops(start, stop):
        @pl.loop(start, stop)
        def _(j):
            ops_high[j], ops_low[j] = split(ops[j])

    ops_copies[0].wait()
    split_ops(0, middle)

    for i in parts:
        from_x(i).wait_recv()
        for step in range(1, n_high):
            go(yz(step, i), has_target)
        if i in through_z:
            go(z(i), has_target)
        for step in range(1, n_high):
            if i < CROSS:
                go(xy(step, i))
        if i < len(through_x):
            pl.when(has_target)(over_z(through_x[i]).wait_recv)
            go(over_x(through_x[i]), has_target)
        for step in range(1, n_high):
            from_y(step, y_order[i]).wait_recv()
            if y_order[i] >= CROSS:
                go(yx(n_high - step, y_order[i]))

    go(to_sibling(1, 0))
    for step in range(1, n_high):
        go(to_sibling(0, n_high - step))

    ops_copies[1].wait()
    split_ops(middle, slots)

    for i in parts:
        one = z(i) if i in through_z else over_x(i)
        pl.when(has_origin)(one.wait_recv)
        go(to_sibling(2, 0, i), has_origin)
        for step in range(1, n_high):
            if i < CROSS:
                from_xy(step, i).wait_recv()
                go(to_sibling(1, n_high - step, i))
            else:
                from_yx(step, i).wait_recv()
                go(to_sibling(1, step, i))
            pl.when(has_origin)(from_yz(step, i).wait_recv)
            go(to_sibling(2, n_high - step, i), has_origin)

    for step in range(n_high):
        from_sibling(0, step).wait_recv()
    from_sibling(1, 0).wait_recv()
    for step in range(1, n_high):
        for i in parts:
            from_sibling(1, step, i).wait_recv()

    @pl.when(has_origin)
    def _():
        for step in range(n_high):
            for i in parts:
                from_sibling(2, step, i).wait_recv()

    for c, when in sent:
        if when is None:
            c.wait_send()
        else:
            pl.when(when)(c.wait_send)


def combine(
    n_sub, src_t, owner, box, ops_high, ops_low, parent_out, owned_out, local_out,
    where_v, where_s, first_rows, second_rows, where_sem,
):
    seg, sub = lax.axis_index("seg"), lax.axis_index("sub")
    rows, width = local_out.shape
    slots = src_t.shape[0]
    tiles = width // LANES
    side = seg % 2
    group_rows = rows * n_sub
    empty_row = 3 * group_rows
    batches = slots // BATCH

    pair_start = (seg - side) * group_rows
    table = jnp.concatenate([src_t[...], jnp.broadcast_to(owner[...], (8, rows))], axis=0)
    local = table - pair_start
    local = jnp.where(local < 0, local + 3 * group_rows, local)
    local = jnp.where(table < 0, empty_row, jnp.clip(local, 0, empty_row))
    where_v[...] = local * tiles
    where_copy = pltpu.make_async_copy(where_v, where_s, where_sem.at[0])
    where_copy.start()

    def spread(ref, start):
        return jnp.concatenate(
            [ref[pl.ds(start + t, rows, stride=tiles), :] for t in range(tiles)], axis=1
        )

    def gather(into, slot, count):
        for i in range(count):
            for r in range(rows):
                at = pl.ds(pl.multiple_of(where_s[slot + i, r], tiles), tiles)
                into[pl.ds((i * rows + r) * tiles, tiles), :] = box[at, :]

    parent_out[...] = spread(box, pl.multiple_of((side * n_sub + sub) * rows * tiles, 8))
    where_copy.wait()
    gather(second_rows, slots, 1)
    owned_out[...] = spread(second_rows, 0)
    gather(first_rows, 0, BATCH)
    local_out[...] = jnp.zeros((rows, width), jnp.float32)

    def translate(rows_of, slot):
        parts = [split(spread(rows_of, i * rows * tiles)) for i in range(BATCH)]
        first = jnp.concatenate([p[0] for p in parts], axis=1)
        second = jnp.concatenate([p[1] for p in parts], axis=1)
        both = jnp.concatenate([first, second], axis=0)
        ops_first = ops_high[pl.ds(slot, BATCH)].reshape(BATCH * width, width)
        ops_second = ops_low[pl.ds(slot, BATCH)].reshape(BATCH * width, width)
        out = jnp.dot(both, ops_first, preferred_element_type=jnp.float32)
        rest = jnp.dot(first, ops_second, preferred_element_type=jnp.float32)
        local_out[...] += out[:rows] + (out[rows:] + rest)

    for b in range(0, batches, 2):
        slot = b * BATCH
        gather(second_rows, slot + BATCH, BATCH)
        translate(first_rows, slot)
        if b + 2 < batches:
            gather(first_rows, slot + 2 * BATCH, BATCH)
        translate(second_rows, slot + BATCH)


def on_device(n_seg, n_sub, leaf_mult, m2m_ops, m2l_ops, owner_box, src_list):
    rows, width = leaf_mult.shape[0] // 8, leaf_mult.shape[1]
    slots = src_list.shape[1]
    n_high = n_sub // 2
    messages = PARTS * (4 + 5 * (n_high - 1)) + 1 + n_high
    group_rows = rows * n_sub
    tiles = width // LANES
    vmem = pl.BlockSpec(memory_space=pltpu.VMEM)
    hbm = pl.BlockSpec(memory_space=pl.ANY)
    half_ops = jax.ShapeDtypeStruct(m2l_ops.shape, jnp.bfloat16)
    box, ops_high, ops_low = pl.pallas_call(
        functools.partial(exchange, n_seg, n_sub),
        out_shape=(
            jax.ShapeDtypeStruct(((3 * group_rows + 8) * tiles, LANES), jnp.float32), half_ops, half_ops
        ),
        in_specs=[hbm, hbm, hbm],
        out_specs=(vmem, vmem, vmem),
        scratch_shapes=[
            pltpu.VMEM((tiles, leaf_mult.shape[0], LANES), jnp.float32),
            pltpu.VMEM(m2m_ops.shape, jnp.float32),
            pltpu.VMEM(m2l_ops.shape, jnp.float32),
            pltpu.VMEM((PARTS, rows // PARTS * tiles, LANES), jnp.float32),
            pltpu.SemaphoreType.DMA((2,)),
            pltpu.SemaphoreType.DMA((tiles,)),
            pltpu.SemaphoreType.DMA((m2m_ops.shape[0],)),
            pltpu.SemaphoreType.DMA((messages,)),
            pltpu.SemaphoreType.DMA((messages,)),
        ],
        compiler_params=pltpu.CompilerParams(
            collective_id=0, has_side_effects=True, vmem_limit_bytes=EXCHANGE_VMEM
        ),
    )(*(pltpu.with_memory_space_constraint(a, pltpu.HBM) for a in (leaf_mult, m2m_ops, m2l_ops)))
    out = jax.ShapeDtypeStruct((rows, width), jnp.float32)
    return pl.pallas_call(
        functools.partial(combine, n_sub),
        out_shape=(out, out, out),
        in_specs=[vmem] * 5,
        out_specs=(vmem, vmem, vmem),
        scratch_shapes=[
            pltpu.VMEM((slots + 8, rows), jnp.int32),
            pltpu.SMEM((slots + 8, rows), jnp.int32),
            pltpu.VMEM((BATCH * rows * tiles, LANES), jnp.float32),
            pltpu.VMEM((BATCH * rows * tiles, LANES), jnp.float32),
            pltpu.SemaphoreType.DMA((1,)),
        ],
        compiler_params=pltpu.CompilerParams(vmem_limit_bytes=COMBINE_VMEM),
    )(src_list.T, owner_box.reshape(1, rows), box, ops_high, ops_low)


def solution(mesh):
    n_seg, n_sub = mesh.shape["seg"], mesh.shape["sub"]
    in_specs = (P(("seg", "sub"), None), P(), P(), P(("seg", "sub")), P(("seg", "sub"), None))
    out_specs = (P(("seg", "sub"), None), P(("seg", "sub"), None), P(("seg", "sub"), None))
    return jax.shard_map(
        functools.partial(on_device, n_seg, n_sub),
        mesh=mesh, in_specs=in_specs, out_specs=out_specs, check_vma=False,
    )
```

```python
import functools

import jax
import jax.numpy as jnp
from jax import lax
from jax.experimental import pallas as pl
from jax.experimental.pallas import tpu as pltpu
from jax.sharding import PartitionSpec as P

MESH = pl.DeviceIdType.MESH
LANES = 128
BATCH = 4
PARTS = 4
DIRECT = 1
CROSS = 1
CHILDREN = 4
EXCHANGE_VMEM = 24 << 20
COMBINE_VMEM = 16 << 20


def split(value):
    high = value.astype(jnp.bfloat16)
    low = (value - high.astype(jnp.float32)).astype(jnp.bfloat16)
    return high, low


def exchange(
    n_seg, n_sub, leaf_hbm, up_hbm, ops_hbm, box, ops_high, ops_low,
    leaf, up, ops, relay, ops_sem, leaf_sem, up_sem, send_sem, recv_sem,
):
    seg, sub = lax.axis_index("seg"), lax.axis_index("sub")
    n_up, width = up.shape[0], up.shape[2]
    slots = ops.shape[0]
    rows = leaf.shape[1] // n_up
    n_high = n_sub // 2
    side, core, high = seg % 2, sub % 2, sub // 2
    partner = seg + 1 - 2 * side
    other_side = 1 - side
    sibling = sub + 1 - 2 * core
    target = seg + 2 - 4 * side
    origin = seg - 2 + 4 * side
    has_target = (target >= 0) & (target < n_seg)
    has_origin = (origin >= 0) & (origin < n_seg)
    tiles = width // LANES
    half = rows // PARTS
    group_rows = rows * n_sub
    empty_row = 3 * group_rows

    leaf_copies = [
        pltpu.make_async_copy(leaf_hbm.at[:, pl.ds(t * LANES, LANES)], leaf.at[t], leaf_sem.at[t])
        for t in range(tiles)
    ]
    for c in leaf_copies:
        c.start()
    middle = slots // 2
    ops_copies = [
        pltpu.make_async_copy(ops_hbm.at[at], ops.at[at], ops_sem.at[k])
        for k, at in enumerate((pl.ds(0, middle), pl.ds(middle, slots - middle)))
    ]

    barrier = pltpu.get_barrier_semaphore()

    def greet(to_seg, to_sub):
        pl.semaphore_signal(barrier, inc=1, device_id=(to_seg, to_sub), device_id_type=MESH)

    def peer(step):
        return lax.rem(high + step, n_high) * 2 + core

    greet(seg, sibling)
    greet(partner, sub)
    for step in range(1, n_high):
        greet(seg, peer(step))

    @pl.when(has_target)
    def _():
        greet(target, sub)
        for step in range(1, n_high):
            greet(target, peer(step))

    @pl.when(has_origin)
    def _():
        greet(origin, sub)
        for step in range(1, n_high):
            greet(origin, peer(step))

    up_copies = [
        pltpu.make_async_copy(
            up_hbm.at[pl.ds(c, CHILDREN)], up.at[pl.ds(c, CHILDREN)], up_sem.at[c // CHILDREN]
        )
        for c in range(0, n_up, CHILDREN)
    ]
    for c in up_copies:
        c.start()

    box[pl.ds(empty_row * tiles, 8 * tiles), :] = jnp.zeros((8 * tiles, LANES), jnp.float32)

    for c in leaf_copies:
        c.wait()
    total = None
    for k, one in enumerate(up_copies):
        one.wait()
        if k == len(up_copies) - 1:
            for c in ops_copies:
                c.start()
        child = jnp.concatenate(
            [
                leaf[t, pl.ds(k * CHILDREN + c, rows, stride=n_up), :]
                for c in range(CHILDREN) for t in range(tiles)
            ],
            axis=1,
        )
        first, second = split(child)
        up_first, up_second = split(up[pl.ds(k * CHILDREN, CHILDREN)].reshape(CHILDREN * width, width))
        both = jnp.concatenate([first, second], axis=0)
        out = jnp.dot(both, up_first, preferred_element_type=jnp.float32)
        rest = jnp.dot(first, up_second, preferred_element_type=jnp.float32)
        term = out[:rows] + (out[rows:] + rest)
        total = term if total is None else total + term
    own_start = pl.multiple_of((side * n_sub + sub) * rows * tiles, 8)
    for t in range(tiles):
        box[pl.ds(own_start + t, rows, stride=tiles), :] = total[:, t * LANES : (t + 1) * LANES]

    pl.semaphore_wait(
        barrier, 1 + n_high + n_high * (has_target.astype(jnp.int32) + has_origin.astype(jnp.int32))
    )

    names = {}

    def copy(name, src, dst, to_seg, to_sub):
        k = names.setdefault(name, len(names))
        return pltpu.make_async_remote_copy(
            src_ref=src, dst_ref=dst, send_sem=send_sem.at[k], recv_sem=recv_sem.at[k],
            device_id=(to_seg, to_sub), device_id_type=MESH,
        )

    def place(group, k, part=None):
        start = (group * n_sub + k) * rows * tiles
        if part is None:
            return box.at[pl.ds(pl.multiple_of(start, 8), rows * tiles)]
        return box.at[pl.ds(pl.multiple_of(start + part * half * tiles, 8), half * tiles)]

    sent = []

    def go(c, when=None):
        sent.append((c, when))
        if when is None:
            c.start()
        else:
            pl.when(when)(c.start)

    def to_x(part):
        at = place(side, sub, part)
        return copy(("x", part), at, at, partner, sub)

    def from_x(part):
        at = place(other_side, sub, part)
        return copy(("x", part), at, at, partner, sub)

    def to_y(step, part):
        at = place(side, sub, part)
        return copy(("y", step, part), at, at, seg, peer(step))

    def from_y(step, part):
        at = place(side, peer(n_high - step), part)
        return copy(("y", step, part), at, at, seg, peer(step))

    def over_z(part):
        return copy(("o", part), place(side, sub, part), relay.at[part], origin, sub)

    def over_x(part):
        return copy(("ox", part), relay.at[part], place(2, sub, part), partner, sub)

    def xy(step, part):
        at = place(other_side, sub, part)
        return copy(("xy", step, part), at, at, seg, peer(step))

    def from_xy(step, part):
        at = place(other_side, peer(n_high - step), part)
        return copy(("xy", step, part), at, at, seg, peer(step))

    def yx(step, part):
        at = place(side, peer(step), part)
        return copy(("yx", step, part), at, at, partner, sub)

    def from_yx(step, part):
        at = place(other_side, peer(step), part)
        return copy(("yx", step, part), at, at, partner, sub)

    def z(part):
        return copy(("z", part), place(other_side, sub, part), place(2, sub, part), target, sub)

    def yz(step, part):
        return copy(
            ("yz", step, part), place(other_side, sub, part), place(2, sub, part), target, peer(step)
        )

    def from_yz(step, part):
        at = place(2, peer(n_high - step), part)
        return copy(("yz", step, part), at, at, target, peer(step))

    def to_sibling(group, step, part=None):
        at = place((side, other_side, 2)[group], peer(step), part)
        return copy(("s", group, step, part), at, at, seg, sibling)

    def from_sibling(group, step, part=None):
        theirs = lax.rem(high + step, n_high) * 2 + 1 - core
        at = place((side, other_side, 2)[group], theirs, part)
        return copy(("s", group, step, part), at, at, seg, sibling)

    parts = list(range(PARTS))
    through_x, through_z = parts[DIRECT:], parts[:DIRECT]
    y_order = parts[CROSS:] + parts[:CROSS]

    for i in parts:
        go(to_x(i))
        for step in range(1, n_high):
            go(to_y(step, y_order[i]))
        if i < len(through_x):
            go(over_z(through_x[i]), has_origin)
    go(to_sibling(0, 0))

    def split_ops(start, stop):
        @pl.loop(start, stop)
        def _(j):
            ops_high[j], ops_low[j] = split(ops[j])

    ops_copies[0].wait()
    split_ops(0, middle)

    for i in parts:
        from_x(i).wait_recv()
        for step in range(1, n_high):
            go(yz(step, i), has_target)
        if i in through_z:
            go(z(i), has_target)
        for step in range(1, n_high):
            if i < CROSS:
                go(xy(step, i))
        if i < len(through_x):
            pl.when(has_target)(over_z(through_x[i]).wait_recv)
            go(over_x(through_x[i]), has_target)
        for step in range(1, n_high):
            from_y(step, y_order[i]).wait_recv()
            if y_order[i] >= CROSS:
                go(yx(n_high - step, y_order[i]))

    go(to_sibling(1, 0))
    for step in range(1, n_high):
        go(to_sibling(0, n_high - step))

    ops_copies[1].wait()
    split_ops(middle, slots)

    for i in parts:
        one = z(i) if i in through_z else over_x(i)
        pl.when(has_origin)(one.wait_recv)
        go(to_sibling(2, 0, i), has_origin)
        for step in range(1, n_high):
            if i < CROSS:
                from_xy(step, i).wait_recv()
                go(to_sibling(1, n_high - step, i))
            else:
                from_yx(step, i).wait_recv()
                go(to_sibling(1, step, i))
            pl.when(has_origin)(from_yz(step, i).wait_recv)
            go(to_sibling(2, n_high - step, i), has_origin)

    for step in range(n_high):
        from_sibling(0, step).wait_recv()
    from_sibling(1, 0).wait_recv()
    for step in range(1, n_high):
        for i in parts:
            from_sibling(1, step, i).wait_recv()

    @pl.when(has_origin)
    def _():
        for step in range(n_high):
            for i in parts:
                from_sibling(2, step, i).wait_recv()

    for c, when in sent:
        if when is None:
            c.wait_send()
        else:
            pl.when(when)(c.wait_send)


def combine(
    n_sub, src_t, owner, box, ops_high, ops_low, parent_out, owned_out, local_out,
    where_v, where_s, first_rows, second_rows, third_rows, where_sem,
):
    seg, sub = lax.axis_index("seg"), lax.axis_index("sub")
    rows, width = local_out.shape
    slots = src_t.shape[0]
    tiles = width // LANES
    side = seg % 2
    group_rows = rows * n_sub
    empty_row = 3 * group_rows
    batches = slots // BATCH

    pair_start = (seg - side) * group_rows
    table = jnp.concatenate([src_t[...], jnp.broadcast_to(owner[...], (8, rows))], axis=0)
    local = table - pair_start
    local = jnp.where(local < 0, local + 3 * group_rows, local)
    local = jnp.where(table < 0, empty_row, jnp.clip(local, 0, empty_row))
    where_v[...] = local * tiles
    early, late = pl.ds(0, 2 * BATCH), pl.ds(2 * BATCH, slots + 8 - 2 * BATCH)
    where_copies = [
        pltpu.make_async_copy(where_v.at[at], where_s.at[at], where_sem.at[k])
        for k, at in enumerate((early, late))
    ]
    for c in where_copies:
        c.start()

    def spread(ref, start):
        return jnp.concatenate(
            [ref[pl.ds(start + t, rows, stride=tiles), :] for t in range(tiles)], axis=1
        )

    def gather(into, slot, count):
        for i in range(count):
            for r in range(rows):
                at = pl.ds(pl.multiple_of(where_s[slot + i, r], tiles), tiles)
                into[pl.ds((i * rows + r) * tiles, tiles), :] = box[at, :]

    parent_out[...] = spread(box, pl.multiple_of((side * n_sub + sub) * rows * tiles, 8))
    where_copies[0].wait()
    gather(first_rows, 0, BATCH)
    where_copies[1].wait()
    gather(third_rows, slots, 1)
    owned_out[...] = spread(third_rows, 0)
    local_out[...] = jnp.zeros((rows, width), jnp.float32)

    def translate(rows_of, slot):
        parts = [split(spread(rows_of, i * rows * tiles)) for i in range(BATCH)]
        first = jnp.concatenate([p[0] for p in parts], axis=1)
        second = jnp.concatenate([p[1] for p in parts], axis=1)
        both = jnp.concatenate([first, second], axis=0)
        ops_first = ops_high[pl.ds(slot, BATCH)].reshape(BATCH * width, width)
        ops_second = ops_low[pl.ds(slot, BATCH)].reshape(BATCH * width, width)
        out = jnp.dot(both, ops_first, preferred_element_type=jnp.float32)
        rest = jnp.dot(first, ops_second, preferred_element_type=jnp.float32)
        local_out[...] += out[:rows] + (out[rows:] + rest)

    for b in range(0, batches, 2):
        slot = b * BATCH
        gather(second_rows, slot + BATCH, BATCH)
        translate(first_rows, slot)
        if b + 2 < batches:
            gather(first_rows, slot + 2 * BATCH, BATCH)
        translate(second_rows, slot + BATCH)


def on_device(n_seg, n_sub, leaf_mult, m2m_ops, m2l_ops, owner_box, src_list):
    rows, width = leaf_mult.shape[0] // 8, leaf_mult.shape[1]
    slots = src_list.shape[1]
    n_high = n_sub // 2
    messages = PARTS * (4 + 5 * (n_high - 1)) + 1 + n_high
    group_rows = rows * n_sub
    tiles = width // LANES
    vmem = pl.BlockSpec(memory_space=pltpu.VMEM)
    hbm = pl.BlockSpec(memory_space=pl.ANY)
    half_ops = jax.ShapeDtypeStruct(m2l_ops.shape, jnp.bfloat16)
    box, ops_high, ops_low = pl.pallas_call(
        functools.partial(exchange, n_seg, n_sub),
        out_shape=(
            jax.ShapeDtypeStruct(((3 * group_rows + 8) * tiles, LANES), jnp.float32), half_ops, half_ops
        ),
        in_specs=[hbm, hbm, hbm],
        out_specs=(vmem, vmem, vmem),
        scratch_shapes=[
            pltpu.VMEM((tiles, leaf_mult.shape[0], LANES), jnp.float32),
            pltpu.VMEM(m2m_ops.shape, jnp.float32),
            pltpu.VMEM(m2l_ops.shape, jnp.float32),
            pltpu.VMEM((PARTS, rows // PARTS * tiles, LANES), jnp.float32),
            pltpu.SemaphoreType.DMA((2,)),
            pltpu.SemaphoreType.DMA((tiles,)),
            pltpu.SemaphoreType.DMA((m2m_ops.shape[0],)),
            pltpu.SemaphoreType.DMA((messages,)),
            pltpu.SemaphoreType.DMA((messages,)),
        ],
        compiler_params=pltpu.CompilerParams(
            collective_id=0, has_side_effects=True, vmem_limit_bytes=EXCHANGE_VMEM
        ),
    )(*(pltpu.with_memory_space_constraint(a, pltpu.HBM) for a in (leaf_mult, m2m_ops, m2l_ops)))
    out = jax.ShapeDtypeStruct((rows, width), jnp.float32)
    return pl.pallas_call(
        functools.partial(combine, n_sub),
        out_shape=(out, out, out),
        in_specs=[vmem] * 5,
        out_specs=(vmem, vmem, vmem),
        scratch_shapes=[
            pltpu.VMEM((slots + 8, rows), jnp.int32),
            pltpu.SMEM((slots + 8, rows), jnp.int32),
            pltpu.VMEM((BATCH * rows * tiles, LANES), jnp.float32),
            pltpu.VMEM((BATCH * rows * tiles, LANES), jnp.float32),
            pltpu.VMEM((rows * tiles, LANES), jnp.float32),
            pltpu.SemaphoreType.DMA((2,)),
        ],
        compiler_params=pltpu.CompilerParams(vmem_limit_bytes=COMBINE_VMEM),
    )(src_list.T, owner_box.reshape(1, rows), box, ops_high, ops_low)


def solution(mesh):
    n_seg, n_sub = mesh.shape["seg"], mesh.shape["sub"]
    in_specs = (P(("seg", "sub"), None), P(), P(), P(("seg", "sub")), P(("seg", "sub"), None))
    out_specs = (P(("seg", "sub"), None), P(("seg", "sub"), None), P(("seg", "sub"), None))
    return jax.shard_map(
        functools.partial(on_device, n_seg, n_sub),
        mesh=mesh, in_specs=in_specs, out_specs=out_specs, check_vma=False,
    )
```
